128 devices in a mesh: dp: 16 (over z, x_lo, core), blk: 8 (over y, x_hi).
Axes of the slice: x: 4 (x_hi: 2, x_lo: 2; x = x_hi * 2 + x_lo), y: 4, z: 4, core: 2. Of those that a mesh axis runs over, the one named last changes fastest.
Arguments:
- features: bfloat16 [32768, 12800], P(('dp', 'blk')), may hold values from -6 to 6
- cotangent: bfloat16 [32768, 12800], P(('dp', 'blk')), may hold values from -6 to 6
- send_order: int32 [128, 256], P(('dp', 'blk')), may hold values from 0 to 255, each once within a row
- pair_index: int32 [384, 2], P(('dp', 'blk')), may hold values from 0 to 1, as said below
- edge_mask: int32 [384, 128, 128], P(('dp', 'blk')), may hold values 0 or 1
- distance: float32 [384, 128, 128], P(('dp', 'blk')), may hold values from 0.8 to 4.8
- radial_weight: float32 [512, 5], replicated, may hold values from -1.5 to 1.5
- mix_weight: bfloat16 [2560, 512], replicated, may hold values from -0.25 to 0.25
- out_weight: bfloat16 [2560, 512], replicated, may hold values from -0.25 to 0.25
Outputs:
- updated: bfloat16 [32768, 12800], P(('dp', 'blk'))
- mix_grad: float32 [2560, 512], P('blk')
- out_grad: float32 [2560, 512], P('blk')
The draws below stay inside these ranges and needn't reach their ends.
Inputs may be any that keep to these rules, and one draw needn't show every extreme that they name: `pair_index`: each device's 3 pairs are distinct; both entries are local block numbers. Each row of send_order is a permutation of the device's rows.
All inputs are finite; a program needn't handle non-finite values. No bound on the sum of `edge_mask` on one device may be relied on, other than what follows from the above.
Results may differ from the reference program's by a relative error of at most 0.0059.
Values may be sent and summed in bfloat16 or wider, within the bound.
A program may use at most 192 MiB of HBM per device.

```python
import math
import jax
import jax.numpy as jnp
import numpy as np
from jax import lax

C = 512
LMAX = 4
LDEG = 25
BLOCK = 128
ROWS = 256
PAIRS = 3
NRBF = 512
WROWS = 2560
ATOMS = 32768
PAIR_ROWS = 384
N_DP = 16
N_BLK = 8
DEVICES = 128


def draw_pair_index(key, part):
    blocks = ROWS // BLOCK
    keys = jax.random.split(key, PAIR_ROWS // PAIRS)
    picks = jax.vmap(lambda one: jax.random.permutation(one, blocks * blocks)[:PAIRS])(keys)
    pairs = jnp.stack([picks // blocks, picks % blocks], axis=-1)
    return pairs.reshape(PAIR_ROWS, 2).astype(jnp.int32)


def plant(values, own_key, low, high):
    spot = [jax.random.randint(jax.random.fold_in(own_key, axis), (), 0, length) for axis, length in enumerate(values.shape)]
    longest = values.shape.index(max(values.shape))
    neighbour = spot[:longest] + [(spot[longest] + 1) % values.shape[longest]] + spot[longest + 1:]
    return values.at[tuple(spot)].set(low).at[tuple(neighbour)].set(high)


def shard_levels(stream_key, shape, shards, smallest, largest):
    def one(axis_at, blocks):
        steps = jax.random.uniform(jax.random.fold_in(jax.random.fold_in(stream_key, 6), axis_at), (blocks,), jnp.float32, smallest / len(shards), largest / len(shards))
        return jnp.repeat(jnp.exp(steps), shape[axis_at] // blocks).reshape((-1,) + (1,) * (len(shape) - axis_at - 1))

    loudness = one(*shards[0])
    for cut in shards[1:]:
        loudness = loudness * one(*cut)
    return loudness


def noise(key, dims, deviation, most, pieces=(), held_as=jnp.bfloat16):
    result = jax.random.normal(key, dims, jnp.float32) * deviation
    if len(pieces) > 0:
        result = shard_levels(key, dims, pieces, -0.22, 0.18) * result
    return jnp.clip(result, min=-most, max=most).astype(held_as)


def setup_inputs(seed: int = 0) -> dict:
    arg_keys = jax.random.split(jax.random.key(seed), 10)
    features = noise(arg_keys[0], (ATOMS, LDEG * C), 1.0, 6.0, ((0, 128),))
    cotangent = noise(arg_keys[1], (ATOMS, LDEG * C), 1.0, 6.0, ((0, 128),))
    send_order = jax.vmap(lambda own: jax.random.permutation(own, ROWS))(jax.random.split(arg_keys[2], DEVICES)).reshape((DEVICES, ROWS)).astype(jnp.int32)
    pair_index = draw_pair_index(jax.random.fold_in(arg_keys[9], 71), 0)
    edge_mask = plant((jax.random.randint(arg_keys[4], (PAIR_ROWS, BLOCK, BLOCK), 0, 4) < 1).astype(jnp.int32), jax.random.fold_in(arg_keys[4], 1), 0, 1)
    distance = jnp.clip(0.8 + 4 * jax.random.uniform(arg_keys[5], (PAIR_ROWS, BLOCK, BLOCK), jnp.float32) ** shard_levels(arg_keys[5], (PAIR_ROWS, BLOCK, BLOCK), ((0, 128),), -0.2, 0.2), 0.8, 4.8)
    radial_weight = noise(arg_keys[6], (NRBF, LMAX + 1), 0.25, 1.5, (), jnp.float32)
    mix_weight = noise(arg_keys[7], (WROWS, C), C ** -0.5, 0.25)
    out_weight = noise(arg_keys[8], (WROWS, C), C ** -0.5, 0.25)
    return {"features": features, "cotangent": cotangent, "send_order": send_order, "pair_index": pair_index, "edge_mask": edge_mask, "distance": distance, "radial_weight": radial_weight, "mix_weight": mix_weight, "out_weight": out_weight}


edge_scale = 0.25
cut_radius = 5.0


def degree_table():
    table = np.zeros((LMAX + 1, LDEG), np.float32)
    for level in range(LMAX + 1):
        table[level, level * level:(level + 1) * (level + 1)] = 1.0
    return table


def gate_one(item, radial_weight):
    mask, dist = item
    centers = cut_radius * jnp.arange(NRBF, dtype=jnp.float32) / (NRBF - 1)
    gamma = 0.5 * ((NRBF - 1) / cut_radius) ** 2
    basis = jnp.exp(-gamma * (dist[..., None] - centers) ** 2)
    radial = jnp.einsum("ijk,kl->ijl", basis, radial_weight, precision=lax.Precision.HIGHEST)
    envelope = 0.5 * (jnp.cos(math.pi * dist / cut_radius) + 1.0) * mask.astype(jnp.float32) * edge_scale
    per_level = radial * envelope[..., None]
    expanded = jnp.einsum("ijl,lk->ijk", per_level, jnp.asarray(degree_table()), precision=lax.Precision.HIGHEST)
    return expanded.astype(jnp.bfloat16)


def gate_of(mask, dist, radial_weight):
    return lax.map(lambda item: gate_one(item, radial_weight), (mask, dist))


def per_degree(rows, weight, form):
    parts = []
    for level in range(LMAX + 1):
        left = rows[:, level * level:(level + 1) * (level + 1)].astype(jnp.float32)
        right = weight[level * C:(level + 1) * C].astype(jnp.float32)
        parts.append(jnp.einsum(form, left, right))
    return jnp.concatenate(parts, axis=1)


def grad_degree(left_rows, right_rows):
    parts = []
    for level in range(LMAX + 1):
        left = left_rows[:, level * level:(level + 1) * (level + 1)].astype(jnp.float32)
        right = right_rows[:, level * level:(level + 1) * (level + 1)].astype(jnp.float32)
        parts.append(jnp.einsum("rkc,rkd->cd", left, right))
    return jnp.concatenate(parts, axis=0)


def device_pass(rows, cot, pairs, mask, dist, radial_weight, mix_weight, out_weight):
    blocks = ROWS // BLOCK
    hidden = rows.reshape(ROWS, LDEG, C)
    grad_rows = cot.reshape(ROWS, LDEG, C)
    gate = gate_of(mask, dist, radial_weight).astype(jnp.float32)
    source = per_degree(hidden, mix_weight, "rkc,cd->rkd").astype(jnp.bfloat16)
    source_blocks = source.reshape(blocks, BLOCK, LDEG, C).astype(jnp.float32)
    gathered = jnp.zeros((blocks, BLOCK, LDEG, C), jnp.float32)
    for pair in range(PAIRS):
        dest, src = pairs[pair, 0], pairs[pair, 1]
        gathered = gathered.at[dest].add(jnp.einsum("ijk,jkc->ikc", gate[pair], source_blocks[src]))
    message = gathered.astype(jnp.bfloat16).reshape(ROWS, LDEG, C)
    mixed = per_degree(message, out_weight, "rkc,cd->rkd")
    updated = (hidden.astype(jnp.float32) + mixed).astype(jnp.bfloat16)
    out_part = grad_degree(message, grad_rows)
    dmessage = per_degree(grad_rows, out_weight, "rkd,cd->rkc").astype(jnp.bfloat16)
    dmessage_blocks = dmessage.reshape(blocks, BLOCK, LDEG, C).astype(jnp.float32)
    dsource = jnp.zeros((blocks, BLOCK, LDEG, C), jnp.float32)
    for pair in range(PAIRS):
        dest, src = pairs[pair, 0], pairs[pair, 1]
        dsource = dsource.at[src].add(jnp.einsum("ijk,ikc->jkc", gate[pair], dmessage_blocks[dest]))
    dsource = dsource.astype(jnp.bfloat16).reshape(ROWS, LDEG, C)
    mix_part = grad_degree(hidden, dsource)
    return updated.reshape(ROWS, LDEG * C), mix_part, out_part


def reference(features, cotangent, send_order, pair_index, edge_mask, distance, radial_weight, mix_weight, out_weight):
    count = N_DP * N_BLK
    width = LDEG * C
    cap = ROWS // N_DP
    grid = features.reshape(N_DP, N_BLK, ROWS, width)
    order = send_order.reshape(N_DP, N_BLK, ROWS, 1).astype(jnp.int32)
    sent = jnp.take_along_axis(grid, order, axis=2)
    moved = sent.reshape(N_DP, N_BLK, N_DP, cap, width).transpose(2, 1, 0, 3, 4).reshape(count, ROWS, width)
    inputs = (moved, cotangent.reshape(count, ROWS, width), pair_index.reshape(count, PAIRS, 2).astype(jnp.int32),
              edge_mask.reshape(count, PAIRS, BLOCK, BLOCK), distance.reshape(count, PAIRS, BLOCK, BLOCK))

    def step(carry, item):
        rows, cot, pairs, mask, dist = item
        updated, mix_part, out_part = device_pass(rows, cot, pairs, mask, dist, radial_weight, mix_weight, out_weight)
        return (carry[0] + mix_part, carry[1] + out_part), updated

    zeros = jnp.zeros((WROWS, C), jnp.float32)
    totals, updated = lax.scan(step, (zeros, zeros), inputs)
    return updated.reshape(ATOMS, width), totals[0], totals[1]
```

```python
import math

import jax
import jax.numpy as jnp
from jax import lax
from jax.experimental import pallas as pl
from jax.experimental.pallas import tpu as pltpu
from jax.sharding import Mesh
from jax.sharding import PartitionSpec as P

LMAX = 4
LDEG = 25
BLOCK = 128
PAIRS = 3
NRBF = 512
C = 512
ROWS = 256
EDGE_ROWS = PAIRS * BLOCK
WROWS = 2560
DP = ("z", "xl", "core")
BLK = ("y", "xh")
MESH = pl.DeviceIdType.MESH

edge_scale = 0.25
cut_radius = 5.0

BF = jnp.bfloat16
F32 = jnp.float32
VM = 56 << 20


def mm(a, b):
    return jnp.dot(a, b, preferred_element_type=F32)


def mm_at(a, b):
    return lax.dot_general(a, b, (((0,), (0,)), ((), ())), preferred_element_type=F32)


def permute_kernel(order_ref, x_ref, o_ref, p_ref):
    @pl.when(pl.program_id(0) == 0)
    def _():
        row = lax.broadcasted_iota(jnp.int32, (ROWS, ROWS), 0)
        hot = jnp.where(row == order_ref[...], 1.0, 0.0).astype(F32)
        p_ref[...] = hot.T.astype(BF)

    o_ref[...] = mm(p_ref[...], x_ref[...]).astype(BF)


def permute(features, order, first, last):
    comps = last - first
    return pl.pallas_call(
        permute_kernel,
        name=f"permute{first}",
        grid=(comps,),
        out_shape=jax.ShapeDtypeStruct((ROWS, comps * C), BF),
        in_specs=[
            pl.BlockSpec((1, ROWS), lambda c: (0, 0)),
            pl.BlockSpec((ROWS, C), lambda c: (0, first + c)),
        ],
        out_specs=pl.BlockSpec((ROWS, C), lambda c: (0, c)),
        scratch_shapes=[pltpu.VMEM((ROWS, ROWS), BF)],
        compiler_params=pltpu.CompilerParams(vmem_limit_bytes=VM),
        cost_estimate=pl.CostEstimate(
            flops=2 * ROWS * ROWS * comps * C, bytes_accessed=4 * ROWS * comps * C, transcendentals=0
        ),
    )(order, features)


def gate_kernel(pair_ref, dist_ref, env_ref, w_ref, g_ref, gt_ref, k_ref, rad_ref):
    scale = math.sqrt(0.5 * math.log2(math.e))
    k_ref[...] = lax.broadcasted_iota(jnp.int32, (NRBF, BLOCK), 0).astype(F32) * scale
    g_ref[...] = jnp.zeros_like(g_ref)
    gt_ref[...] = jnp.zeros_like(gt_ref)
    weight = w_ref[...]

    def step(at, carry):
        base = at * 8
        rows = dist_ref[pl.ds(pl.multiple_of(base, 8), 8), :] * ((NRBF - 1) / cut_radius * scale)
        for two in range(4):
            halves = []
            for one in range(2):
                spot = two * 2 + one
                off = rows[spot : spot + 1, :] - k_ref[...]
                halves.append(jnp.exp2(-(off * off)).astype(BF))
            basis = jnp.concatenate(halves, axis=1)
            both = mm(weight, basis)
            total = both[:8] + both[8:]
            for one in range(2):
                spot = two * 2 + one
                rad_ref[pl.ds(pl.multiple_of((base + spot) * 8, 8), 8), :] = total[
                    :, one * BLOCK : (one + 1) * BLOCK
                ]
        return carry

    lax.fori_loop(0, EDGE_ROWS // 8, step, 0)
    for pair in range(PAIRS):
        dest = pl.multiple_of(pair_ref[pair, 0] * BLOCK, BLOCK)
        src = pl.multiple_of(pair_ref[pair, 1] * BLOCK, BLOCK)
        env = env_ref[pair * BLOCK : (pair + 1) * BLOCK, :]
        for level in range(LMAX + 1):
            radial = rad_ref[pl.ds(pair * BLOCK * 8 + level, BLOCK, stride=8), :]
            gate = radial * env
            g_ref[level, pl.ds(dest, BLOCK), pl.ds(src, BLOCK)] = gate.astype(BF)
            gt_ref[level, pl.ds(src, BLOCK), pl.ds(dest, BLOCK)] = gate.T.astype(BF)


def gates(pair_index, edge_mask, distance, radial_weight):
    dist = distance.reshape(EDGE_ROWS, BLOCK)
    mask = edge_mask.reshape(EDGE_ROWS, BLOCK)
    env = 0.5 * (jnp.cos(math.pi * dist / cut_radius) + 1.0) * mask.astype(F32) * edge_scale
    weight = jnp.pad(radial_weight.T, ((0, 3), (0, 0)))
    high = weight.astype(BF)
    low = (weight - high.astype(F32)).astype(BF)
    split = jnp.concatenate([high, low], axis=0)
    vmem = pl.BlockSpec(memory_space=pltpu.VMEM)
    shape = jax.ShapeDtypeStruct((LMAX + 1, ROWS, ROWS), BF)
    return pl.pallas_call(
        gate_kernel,
        name="gate",
        out_shape=(shape, shape),
        in_specs=[pl.BlockSpec(memory_space=pltpu.SMEM), vmem, vmem, vmem],
        out_specs=(vmem, vmem),
        scratch_shapes=[pltpu.VMEM((NRBF, BLOCK), F32), pltpu.VMEM((EDGE_ROWS * 8, BLOCK), F32)],
        compiler_params=pltpu.CompilerParams(vmem_limit_bytes=VM),
        cost_estimate=pl.CostEstimate(
            flops=2 * EDGE_ROWS * BLOCK * NRBF * 256, bytes_accessed=2 << 20, transcendentals=EDGE_ROWS * BLOCK * NRBF
        ),
    )(pair_index, dist, env, split)


def level_of(comp):
    return sum((comp >= level * level).astype(jnp.int32) for level in range(1, LMAX + 1))


def dsource_kernel(cot_ref, v_ref, gt_ref, o_ref):
    dmessage = mm(cot_ref[...], v_ref[...]).astype(BF)
    o_ref[...] = mm(gt_ref[0], dmessage).astype(BF)


def dsources(cotangent, out_weight, gt):
    turned = jnp.swapaxes(out_weight.reshape(LMAX + 1, C, C), 1, 2).reshape(WROWS, C)
    return pl.pallas_call(
        dsource_kernel,
        name="dsource",
        grid=(LDEG,),
        out_shape=jax.ShapeDtypeStruct((ROWS, LDEG * C), BF),
        in_specs=[
            pl.BlockSpec((ROWS, C), lambda c: (0, c)),
            pl.BlockSpec((C, C), lambda c: (level_of(c), 0)),
            pl.BlockSpec((1, ROWS, ROWS), lambda c: (level_of(c), 0, 0)),
        ],
        out_specs=pl.BlockSpec((ROWS, C), lambda c: (0, c)),
        compiler_params=pltpu.CompilerParams(vmem_limit_bytes=VM),
        cost_estimate=pl.CostEstimate(
            flops=2 * ROWS * C * (C + ROWS) * LDEG, bytes_accessed=4 * ROWS * C * LDEG, transcendentals=0
        ),
    )(cotangent, turned, gt)


def layer_kernel(last, x_ref, cot_ref, ds_ref, w_ref, v_ref, g_ref, *rest):
    u_ref, grad_ref, mix_acc, out_acc = rest[-4:]
    comp = pl.program_id(0)

    @pl.when(comp == 0)
    def _():
        mix_acc[...] = jnp.zeros_like(mix_acc)
        out_acc[...] = jnp.zeros_like(out_acc)

    hidden = x_ref[...]
    source = mm(hidden, w_ref[...]).astype(BF)
    message = mm(g_ref[0], source).astype(BF)
    u_ref[...] = (hidden.astype(F32) + mm(message, v_ref[...])).astype(BF)
    out_acc[...] += mm_at(message, cot_ref[...])
    mix_acc[...] += mm_at(hidden, ds_ref[...])

    @pl.when(comp == last)
    def _():
        grad_ref[0] = mix_acc[...].astype(BF)
        grad_ref[1] = out_acc[...].astype(BF)


def layer(level, hidden, first, cotangent, dsource, mix_weight, out_weight, g, held):
    comps = 2 * level + 1
    start = level * level
    args = [hidden, cotangent, dsource, mix_weight, out_weight, g]
    specs = [
        pl.BlockSpec((ROWS, C), lambda c: (0, start - first + c)),
        pl.BlockSpec((ROWS, C), lambda c: (0, start + c)),
        pl.BlockSpec((ROWS, C), lambda c: (0, start + c)),
        pl.BlockSpec((C, C), lambda c: (level, 0)),
        pl.BlockSpec((C, C), lambda c: (level, 0)),
        pl.BlockSpec((1, ROWS, ROWS), lambda c: (level, 0, 0)),
    ]
    alias = {}
    if held is not None:
        args.extend(held)
        specs.extend([pl.BlockSpec(memory_space=pl.ANY)] * 2)
        alias = {6: 0, 7: 1}

    def kernel(*refs):
        layer_kernel(comps - 1, *refs)

    return pl.pallas_call(
        kernel,
        name=f"layer{level}",
        grid=(comps,),
        out_shape=(
            jax.ShapeDtypeStruct((ROWS, LDEG * C), BF),
            jax.ShapeDtypeStruct((2, WROWS, C), BF),
        ),
        in_specs=specs,
        out_specs=(
            pl.BlockSpec((ROWS, C), lambda c: (0, start + c)),
            pl.BlockSpec((2, C, C), lambda c: (0, level, 0)),
        ),
        scratch_shapes=[pltpu.VMEM((C, C), F32), pltpu.VMEM((C, C), F32)],
        input_output_aliases=alias,
        compiler_params=pltpu.CompilerParams(vmem_limit_bytes=VM),
        cost_estimate=pl.CostEstimate(
            flops=2 * ROWS * C * (4 * C + ROWS) * comps, bytes_accessed=8 * ROWS * C * comps, transcendentals=0
        ),
    )(*args)


def exchange(x, axis):
    return lax.all_to_all(x, axis, split_axis=0, concat_axis=0, tiled=True)


def remote(src, dst, send, recv, where):
    return pltpu.make_async_remote_copy(
        src_ref=src, dst_ref=dst, send_sem=send, recv_sem=recv, device_id=where, device_id_type=MESH
    )


def sum_kernel(g_ref, o_ref, ra, sb, rb, sc, own, rc, fin, a_s, a_r, b_s, b_r, c_s, c_r, d_s, d_r, e_s, e_r):
    z, xl, core = lax.axis_index("z"), lax.axis_index("xl"), lax.axis_index("core")
    y, xh = lax.axis_index("y"), lax.axis_index("xh")
    x = xh * 2 + xl
    levels = range(LMAX, -1, -1)

    def copy_a(level):
        return remote(
            g_ref.at[1 - core, pl.ds(level * C, C)], ra.at[level], a_s.at[level], a_r.at[level], {"core": 1 - core}
        )

    def copy_b(level, j):
        to = lax.rem(y + j, 4)
        return remote(
            sb.at[level, pl.ds(pl.multiple_of(to * 128, 128), 128)],
            rb.at[level, j - 1],
            b_s.at[level, j - 1],
            b_r.at[level, j - 1],
            {"y": to},
        )

    def copy_c(k):
        to_z, to_x = lax.rem(z + k // 4, 4), lax.rem(x + k % 4, 4)
        return remote(
            sc.at[:, pl.ds(pl.multiple_of(to_z * 32, 32), 32), pl.ds(pl.multiple_of(to_x * 128, 128), 128)],
            rc.at[k - 1],
            c_s.at[k - 1],
            c_r.at[k - 1],
            {"z": to_z, "xl": lax.rem(to_x, 2), "xh": to_x // 2},
        )

    for level in levels:
        copy_a(level).start()
    for level in levels:
        copy_a(level).wait()
        sb[level] = (g_ref[core, pl.ds(level * C, C)].astype(F32) + ra[level].astype(F32)).astype(BF)
        for j in (2, 1, 3):
            copy_b(level, j).start()
    for level in levels:
        for j in (1, 3, 2):
            copy_b(level, j).wait()
        rows = pl.multiple_of(y * 128, 128)
        total = g_ref[core, pl.ds(level * C + rows, 128)].astype(F32) + ra[level, pl.ds(rows, 128)].astype(F32)
        for j in range(3):
            total = total + rb[level, j].astype(F32)
        own[level] = total
        sc[level] = total.astype(BF)
    for k in range(1, 16):
        copy_c(k).start()
    total = own[:, pl.ds(pl.multiple_of(z * 32, 32), 32), pl.ds(pl.multiple_of(x * 128, 128), 128)]
    for k in range(1, 16):
        copy_c(k).wait()
        total = total + rc[k - 1].astype(F32)
    fin[...] = total

    def piece(level, act):
        group = level * 16 + y * 4 + z
        blk = group // 10
        to_y, to_xh = blk // 2, lax.rem(blk, 2)
        rows = pl.multiple_of(lax.rem(group, 10) * 32, 32)
        dst = o_ref.at[core, pl.ds(rows, 32), pl.ds(pl.multiple_of(x * 128, 128), 128)]
        here = jnp.logical_and(to_y == y, to_xh == xh)
        for k in range(8):
            where = {"z": lax.rem(z + k // 2, 4), "xl": lax.rem(xl + k % 2, 2), "y": to_y, "xh": to_xh}
            copy = remote(fin.at[level], dst, d_s.at[level, k], d_r, where)
            if k:
                act(copy)
            else:
                pl.when(jnp.logical_not(here))(lambda: act(copy))
        return here, dst

    for level in levels:
        here, dst = piece(level, lambda copy: copy.start())
        pl.when(here)(lambda: pltpu.make_async_copy(fin.at[level], dst, d_r).start())
    pltpu.make_async_copy(o_ref.at[core], o_ref.at[core], d_r).wait()
    last = remote(o_ref.at[core], o_ref.at[core], e_s, e_r, {"core": 1 - core})
    last.start()
    for level in levels:
        piece(level, lambda copy: copy.wait_send())
    last.wait()


def reduce_grads(grads):
    dma = pltpu.SemaphoreType.DMA
    n = LMAX + 1
    full = pl.pallas_call(
        sum_kernel,
        name="sum_grads",
        out_shape=jax.ShapeDtypeStruct((2, 320, C), F32),
        in_specs=[pl.BlockSpec(memory_space=pltpu.VMEM)],
        out_specs=pl.BlockSpec(memory_space=pltpu.VMEM),
        scratch_shapes=[
            pltpu.VMEM((n, C, C), BF),
            pltpu.VMEM((n, C, C), BF),
            pltpu.VMEM((n, 3, 128, C), BF),
            pltpu.VMEM((n, 128, C), BF),
            pltpu.VMEM((n, 128, C), F32),
            pltpu.VMEM((15, n, 32, 128), BF),
            pltpu.VMEM((n, 32, 128), F32),
            dma((n,)),
            dma((n,)),
            dma((n, 3)),
            dma((n, 3)),
            dma((15,)),
            dma((15,)),
            dma((n, 8)),
            dma,
            dma,
            dma,
        ],
        compiler_params=pltpu.CompilerParams(has_side_effects=True, vmem_limit_bytes=VM),
    )(grads)
    return full[0], full[1]


def after(x, *others):
    return lax.optimization_barrier((x, *others))[0]


def body(
    features,
    cotangent,
    send_order,
    pair_index,
    edge_mask,
    distance,
    radial_weight,
    mix_weight,
    out_weight,
):
    local = {}
    chunks = ((16, 25), (9, 16), (0, 9))
    order, sent, previous = send_order, [], None
    for first, last in chunks:
        rows = permute(features, order, first, last)
        order = after(order, rows)
        sent.append(rows)
    for (first, last), rows in zip(chunks, sent):
        if previous is not None:
            rows = after(rows, previous)
        previous = exchange(rows, DP)
        for comp in range(first, last):
            local[comp] = (previous, first)
    g, gt = gates(pair_index, edge_mask, distance, radial_weight)
    dsource = dsources(cotangent, out_weight, gt)
    held = None
    for level in range(LMAX, -1, -1):
        held = layer(level, *local[level * level], cotangent, dsource, mix_weight, out_weight, g, held)
    updated, grads = held
    mix_grad, out_grad = reduce_grads(grads)
    return updated, mix_grad, out_grad


def solution(mesh):
    split = Mesh(mesh.devices.reshape(4, 2, 2, 4, 2), DP + BLK)
    rows = P(DP + BLK, None)
    cubes = P(DP + BLK, None, None)
    return jax.shard_map(
        body,
        mesh=split,
        in_specs=(rows, rows, rows, rows, cubes, cubes, P(), P(), P()),
        out_specs=(rows, P(BLK, None), P(BLK, None)),
        check_vma=False,
    )
```

```python
import math

import jax
import jax.numpy as jnp
from jax import lax
from jax.experimental import pallas as pl
from jax.experimental.pallas import tpu as pltpu
from jax.sharding import Mesh
from jax.sharding import PartitionSpec as P

LMAX = 4
LDEG = 25
BLOCK = 128
PAIRS = 3
NRBF = 512
C = 512
ROWS = 256
EDGE_ROWS = PAIRS * BLOCK
WROWS = 2560
DP = ("z", "xl", "core")
BLK = ("y", "xh")
MESH = pl.DeviceIdType.MESH

edge_scale = 0.25
cut_radius = 5.0

BF = jnp.bfloat16
F32 = jnp.float32
VM = 56 << 20


def mm(a, b):
    return jnp.dot(a, b, preferred_element_type=F32)


def mm_bt(a, b):
    return lax.dot_general(a, b, (((1,), (1,)), ((), ())), preferred_element_type=F32)


def mm_at(a, b):
    return lax.dot_general(a, b, (((0,), (0,)), ((), ())), preferred_element_type=F32)


def permute_kernel(order_ref, x_ref, o_ref, p_ref):
    @pl.when(pl.program_id(0) == 0)
    def _():
        row = lax.broadcasted_iota(jnp.int32, (ROWS, ROWS), 0)
        hot = jnp.where(row == order_ref[...], 1.0, 0.0).astype(F32)
        p_ref[...] = hot.T.astype(BF)

    o_ref[...] = mm(p_ref[...], x_ref[...]).astype(BF)


def permute(features, order):
    width = 5 * C
    return pl.pallas_call(
        permute_kernel,
        name="permute",
        grid=(LDEG * C // width,),
        out_shape=jax.ShapeDtypeStruct((ROWS, LDEG * C), BF),
        in_specs=[
            pl.BlockSpec((1, ROWS), lambda c: (0, 0)),
            pl.BlockSpec((ROWS, width), lambda c: (0, c)),
        ],
        out_specs=pl.BlockSpec((ROWS, width), lambda c: (0, c)),
        scratch_shapes=[pltpu.VMEM((ROWS, ROWS), BF)],
        compiler_params=pltpu.CompilerParams(vmem_limit_bytes=VM),
    )(order, features)


def remote(src, dst, send, recv, where):
    return pltpu.make_async_remote_copy(
        src_ref=src, dst_ref=dst, send_sem=send, recv_sem=recv, device_id=where, device_id_type=MESH
    )


def gate_sums(dist_ref, w_ref, k_ref, rad_ref):
    scale = math.sqrt(0.5 * math.log2(math.e))
    k_ref[...] = lax.broadcasted_iota(jnp.int32, (NRBF, BLOCK), 0).astype(F32) * scale
    weight = w_ref[...]

    def step(at, carry):
        base = at * 8
        rows = dist_ref[pl.ds(pl.multiple_of(base, 8), 8), :] * ((NRBF - 1) / cut_radius * scale)
        for two in range(4):
            high, low = [], []
            for one in range(2):
                spot = two * 2 + one
                off = rows[spot : spot + 1, :] - k_ref[...]
                basis = jnp.exp2(-(off * off))
                top = basis.astype(BF)
                high.append(top)
                low.append((basis - top.astype(F32)).astype(BF))
            both = mm(weight, jnp.concatenate([jnp.concatenate(high, axis=1), jnp.concatenate(low, axis=1)], axis=0))
            total = both[:8] + both[8:]
            for one in range(2):
                spot = two * 2 + one
                rad_ref[pl.ds(pl.multiple_of((base + spot) * 8, 8), 8), :] = total[
                    :, one * BLOCK : (one + 1) * BLOCK
                ]
        return carry

    lax.fori_loop(0, EDGE_ROWS // 8, step, 0)


def gate_blocks(sel_ref, env_ref, rad_ref, g_ref, gt_ref):
    for level in range(LMAX + 1):
        gate = [
            rad_ref[pl.ds(pair * BLOCK * 8 + level, BLOCK, stride=8), :]
            * env_ref[pair * BLOCK : (pair + 1) * BLOCK, :]
            for pair in range(PAIRS)
        ]
        for dest in range(2):
            for src in range(2):
                spot = (dest * 2 + src) * PAIRS
                block = sum(sel_ref[spot + pair] * gate[pair] for pair in range(PAIRS))
                rows, cols = slice(dest * BLOCK, (dest + 1) * BLOCK), slice(src * BLOCK, (src + 1) * BLOCK)
                g_ref[level, rows, cols] = block.astype(BF)
                gt_ref[level, cols, rows] = block.T.astype(BF)


def layer_kernel(
    sel_ref, dist_ref, env_ref, wt_ref, h_ref, cot_hbm, w_hbm, v_hbm, u_hbm, o_ref,
    x_ref, cot_ref, ds_ref, w_ref, v_ref, g_ref, gt_ref, k_ref, rad_ref, mix_acc, out_acc, grads,
    ra, sb, rb, sc, own, rc, fin,
    h_s, h_r, i_s, cot_s, w_s, u_s, a_s, a_r, b_s, b_r, c_s, c_r, d_s, d_r, e_s, e_r,
):
    z, xl, core = lax.axis_index("z"), lax.axis_index("xl"), lax.axis_index("core")
    y, xh = lax.axis_index("y"), lax.axis_index("xh")
    x = xh * 2 + xl
    levels = range(LMAX, -1, -1)

    def copy_a(level):
        return remote(
            grads.at[1 - core, pl.ds(level * C, C)], ra.at[level], a_s.at[level], a_r.at[level], {"core": 1 - core}
        )

    def copy_b(level, j):
        to = lax.rem(y + j, 4)
        return remote(
            sb.at[level, pl.ds(pl.multiple_of(to * 128, 128), 128)],
            rb.at[level, j - 1],
            b_s.at[level, j - 1],
            b_r.at[level, j - 1],
            {"y": to},
        )

    def copy_c(k):
        to_z, to_x = lax.rem(z + k // 4, 4), lax.rem(x + k % 4, 4)
        return remote(
            sc.at[:, pl.ds(pl.multiple_of(to_z * 32, 32), 32), pl.ds(pl.multiple_of(to_x * 128, 128), 128)],
            rc.at[k - 1],
            c_s.at[k - 1],
            c_r.at[k - 1],
            {"z": to_z, "xl": lax.rem(to_x, 2), "xh": to_x // 2},
        )

    me = (z * 2 + xl) * 2 + core

    def part(level):
        return pl.ds(level * level * C, (2 * level + 1) * C)

    def copy_h(level, k):
        to = lax.rem(me + k, 16)
        return remote(
            h_ref.at[pl.ds(pl.multiple_of(to * 16, 16), 16), part(level)],
            x_ref.at[pl.ds(pl.multiple_of(me * 16, 16), 16), part(level)],
            h_s.at[level, k - 1],
            h_r.at[level, k - 1],
            {"z": to // 4, "xl": lax.rem(to // 2, 2), "core": lax.rem(to, 2)},
        )

    def stay_h(level):
        rows = pl.ds(pl.multiple_of(me * 16, 16), 16)
        return pltpu.make_async_copy(h_ref.at[rows, part(level)], x_ref.at[rows, part(level)], i_s.at[level])

    cot_in = pltpu.make_async_copy(cot_hbm, cot_ref, cot_s)
    w_in = pltpu.make_async_copy(w_hbm, w_ref, w_s.at[0])
    v_in = pltpu.make_async_copy(v_hbm, v_ref, w_s.at[1])

    def copy_u(level):
        return pltpu.make_async_copy(x_ref.at[:, part(level)], u_hbm.at[:, part(level)], u_s.at[level])

    for level in levels:
        for k in range(1, 16):
            copy_h(level, k).start()
        stay_h(level).start()
    cot_in.start()
    v_in.start()
    w_in.start()

    gate_sums(dist_ref, wt_ref, k_ref, rad_ref)
    gate_blocks(sel_ref, env_ref, rad_ref, g_ref, gt_ref)
    cot_in.wait()
    v_in.wait()
    w_in.wait()

    def comp_columns(comp):
        return pl.ds(pl.multiple_of(comp * C, C), C)

    for level in levels:

        def dsource(comp, carry):
            cols = comp_columns(comp)
            dmessage = mm_bt(cot_ref[:, cols], v_ref[pl.ds(level * C, C), :]).astype(BF)
            ds_ref[:, cols] = mm(gt_ref[level], dmessage).astype(BF)
            return carry

        lax.fori_loop(level * level, (level + 1) * (level + 1), dsource, 0)

    def finish_a(level):
        copy_a(level).wait()
        sb[level] = (grads[core, pl.ds(level * C, C)].astype(F32) + ra[level].astype(F32)).astype(BF)
        for j in (2, 1, 3):
            copy_b(level, j).start()

    def finish_b(level):
        for j in (1, 3, 2):
            copy_b(level, j).wait()
        rows = pl.multiple_of(y * 128, 128)
        total = grads[core, pl.ds(level * C + rows, 128)].astype(F32) + ra[level, pl.ds(rows, 128)].astype(F32)
        for j in range(3):
            total = total + rb[level, j].astype(F32)
        own[level] = total
        sc[level] = total.astype(BF)

    for level in levels:
        stay_h(level).wait()
        for k in range(1, 16):
            copy_h(level, k).wait_recv()
        mix_acc[...] = jnp.zeros_like(mix_acc)
        out_acc[...] = jnp.zeros_like(out_acc)

        def forward(comp, carry):
            cols = comp_columns(comp)
            hidden = x_ref[:, cols]
            source = mm(hidden, w_ref[pl.ds(level * C, C), :]).astype(BF)
            message = mm(g_ref[level], source).astype(BF)
            mixed = mm(message, v_ref[pl.ds(level * C, C), :])
            mix_acc[...] += mm_at(hidden, ds_ref[:, cols])
            out_acc[...] += mm_at(message, cot_ref[:, cols])
            x_ref[:, cols] = (hidden.astype(F32) + mixed).astype(BF)
            return carry

        lax.fori_loop(level * level, (level + 1) * (level + 1), forward, 0)
        copy_u(level).start()
        grads[0, pl.ds(level * C, C)] = mix_acc[...].astype(BF)
        grads[1, pl.ds(level * C, C)] = out_acc[...].astype(BF)
        copy_a(level).start()
        if level < LMAX:
            finish_a(level + 1)
        if level < LMAX - 1:
            finish_b(level + 2)
    finish_a(0)
    finish_b(1)
    finish_b(0)
    for k in range(1, 16):
        copy_c(k).start()
    total = own[:, pl.ds(pl.multiple_of(z * 32, 32), 32), pl.ds(pl.multiple_of(x * 128, 128), 128)]
    for k in range(1, 16):
        copy_c(k).wait()
        total = total + rc[k - 1].astype(F32)
    fin[...] = total

    def piece(level, act):
        group = level * 16 + y * 4 + z
        blk = group // 10
        to_y, to_xh = blk // 2, lax.rem(blk, 2)
        rows = pl.multiple_of(lax.rem(group, 10) * 32, 32)
        dst = o_ref.at[core, pl.ds(rows, 32), pl.ds(pl.multiple_of(x * 128, 128), 128)]
        here = jnp.logical_and(to_y == y, to_xh == xh)
        for k in range(8):
            where = {"z": lax.rem(z + k // 2, 4), "xl": lax.rem(xl + k % 2, 2), "y": to_y, "xh": to_xh}
            copy = remote(fin.at[level], dst, d_s.at[level, k], d_r, where)
            if k:
                act(copy)
            else:
                pl.when(jnp.logical_not(here))(lambda: act(copy))
        return here, dst

    for level in levels:
        here, dst = piece(level, lambda copy: copy.start())
        pl.when(here)(lambda: pltpu.make_async_copy(fin.at[level], dst, d_r).start())
    pltpu.make_async_copy(o_ref.at[core], o_ref.at[core], d_r).wait()
    last = remote(o_ref.at[core], o_ref.at[core], e_s, e_r, {"core": 1 - core})
    last.start()
    for level in levels:
        piece(level, lambda copy: copy.wait_send())
    last.wait()
    for level in levels:
        copy_u(level).wait()
        for k in range(1, 16):
            copy_h(level, k).wait_send()


def run_layer(sel, dist, env, split, rows, cotangent, mix_weight, out_weight):
    dma = pltpu.SemaphoreType.DMA
    n = LMAX + 1
    vmem, hbm = pl.BlockSpec(memory_space=pltpu.VMEM), pl.BlockSpec(memory_space=pl.ANY)
    updated, full = pl.pallas_call(
        layer_kernel,
        name="layer",
        out_shape=(
            jax.ShapeDtypeStruct((ROWS, LDEG * C), BF),
            jax.ShapeDtypeStruct((2, 320, C), F32),
        ),
        in_specs=[pl.BlockSpec(memory_space=pltpu.SMEM), vmem, vmem, vmem, hbm, hbm, hbm, hbm],
        out_specs=(hbm, vmem),
        scratch_shapes=[
            pltpu.VMEM((ROWS, LDEG * C), BF),
            pltpu.VMEM((ROWS, LDEG * C), BF),
            pltpu.VMEM((ROWS, LDEG * C), BF),
            pltpu.VMEM((WROWS, C), BF),
            pltpu.VMEM((WROWS, C), BF),
            pltpu.VMEM((n, ROWS, ROWS), BF),
            pltpu.VMEM((n, ROWS, ROWS), BF),
            pltpu.VMEM((NRBF, BLOCK), F32),
            pltpu.VMEM((EDGE_ROWS * 8, BLOCK), F32),
            pltpu.VMEM((C, C), F32),
            pltpu.VMEM((C, C), F32),
            pltpu.VMEM((2, WROWS, C), BF),
            pltpu.VMEM((n, C, C), BF),
            pltpu.VMEM((n, C, C), BF),
            pltpu.VMEM((n, 3, 128, C), BF),
            pltpu.VMEM((n, 128, C), BF),
            pltpu.VMEM((n, 128, C), F32),
            pltpu.VMEM((15, n, 32, 128), BF),
            pltpu.VMEM((n, 32, 128), F32),
            dma((n, 15)),
            dma((n, 15)),
            dma((n,)),
            dma,
            dma((2,)),
            dma((n,)),
            dma((n,)),
            dma((n,)),
            dma((n, 3)),
            dma((n, 3)),
            dma((15,)),
            dma((15,)),
            dma((n, 8)),
            dma,
            dma,
            dma,
        ],
        compiler_params=pltpu.CompilerParams(has_side_effects=True, vmem_limit_bytes=VM),
    )(sel, dist, env, split, rows, cotangent, mix_weight, out_weight)
    return updated, full[0], full[1]


def body(
    features,
    cotangent,
    send_order,
    pair_index,
    edge_mask,
    distance,
    radial_weight,
    mix_weight,
    out_weight,
):
    rows = permute(features, send_order)
    dist = distance.reshape(EDGE_ROWS, BLOCK)
    mask = edge_mask.reshape(EDGE_ROWS, BLOCK)
    env = 0.5 * (jnp.cos(math.pi * dist / cut_radius) + 1.0) * mask.astype(F32) * edge_scale
    weight = jnp.pad(radial_weight.T, ((0, 3), (0, 0)))
    high = weight.astype(BF)
    low = (weight - high.astype(F32)).astype(BF)
    split = jnp.block([[high, high], [low, jnp.zeros_like(low)]])
    spot = pair_index[:, 0] * 2 + pair_index[:, 1]
    sel = (jnp.arange(4)[:, None] == spot[None, :]).astype(F32).reshape(4 * PAIRS)
    return run_layer(sel, dist, env, split, rows, cotangent, mix_weight, out_weight)


def solution(mesh):
    split = Mesh(mesh.devices.reshape(4, 2, 2, 4, 2), DP + BLK)
    rows = P(DP + BLK, None)
    cubes = P(DP + BLK, None, None)
    return jax.shard_map(
        body,
        mesh=split,
        in_specs=(rows, rows, rows, rows, cubes, cubes, P(), P(), P()),
        out_specs=(rows, P(BLK, None), P(BLK, None)),
        check_vma=False,
    )
```

```python
import math

import jax
import jax.numpy as jnp
from jax import lax
from jax.experimental import pallas as pl
from jax.experimental.pallas import tpu as pltpu
from jax.sharding import Mesh
from jax.sharding import PartitionSpec as P

LMAX = 4
LDEG = 25
BLOCK = 128
PAIRS = 3
NRBF = 512
C = 512
ROWS = 256
EDGE_ROWS = PAIRS * BLOCK
WROWS = 2560
DP = ("z", "xl", "core")
BLK = ("y", "xh")
MESH = pl.DeviceIdType.MESH

edge_scale = 0.25
cut_radius = 5.0

BF = jnp.bfloat16
F32 = jnp.float32
VM = 56 << 20


def mm(a, b):
    return jnp.dot(a, b, preferred_element_type=F32)


def mm_bt(a, b):
    return lax.dot_general(a, b, (((1,), (1,)), ((), ())), preferred_element_type=F32)


def mm_at(a, b):
    return lax.dot_general(a, b, (((0,), (0,)), ((), ())), preferred_element_type=F32)


def remote(src, dst, send, recv, where):
    return pltpu.make_async_remote_copy(
        src_ref=src, dst_ref=dst, send_sem=send, recv_sem=recv, device_id=where, device_id_type=MESH
    )


def gate_sums(dist_ref, radial_ref, turn_ref, k_ref, rad_ref):
    scale = math.sqrt(0.5 * math.log2(math.e))
    k_ref[...] = lax.broadcasted_iota(jnp.int32, (NRBF, BLOCK), 0).astype(F32) * scale
    turn_ref[...] = jnp.zeros_like(turn_ref)
    turn_ref[: LMAX + 1, :] = radial_ref[...]
    radial = turn_ref[...]
    high_w = radial.astype(BF)
    low_w = (radial - high_w.astype(F32)).astype(BF)
    weight = jnp.concatenate(
        [
            jnp.concatenate([high_w, high_w], axis=1).astype(F32),
            jnp.concatenate([low_w, jnp.zeros_like(low_w)], axis=1).astype(F32),
        ],
        axis=0,
    ).astype(BF)

    def step(at, carry):
        base = at * 8
        rows = dist_ref[pl.ds(pl.multiple_of(base, 8), 8), :] * ((NRBF - 1) / cut_radius * scale)
        for two in range(4):
            high, low = [], []
            for one in range(2):
                spot = two * 2 + one
                off = rows[spot : spot + 1, :] - k_ref[...]
                basis = jnp.exp2(-(off * off))
                top = basis.astype(BF)
                high.append(top)
                low.append((basis - top.astype(F32)).astype(BF))
            both = mm(weight, jnp.concatenate([jnp.concatenate(high, axis=1), jnp.concatenate(low, axis=1)], axis=0))
            total = both[:8] + both[8:]
            for one in range(2):
                spot = two * 2 + one
                rad_ref[pl.ds(pl.multiple_of((base + spot) * 8, 8), 8), :] = total[
                    :, one * BLOCK : (one + 1) * BLOCK
                ]
        return carry

    lax.fori_loop(0, EDGE_ROWS // 8, step, 0)


def gate_blocks(pair_ref, dist_ref, mask_ref, env_ref, rad_ref, g_ref, gt_ref):
    env_ref[...] = (
        0.5 * (jnp.cos(math.pi * dist_ref[...] / cut_radius) + 1.0) * mask_ref[...].astype(F32) * edge_scale
    )
    for level in range(LMAX + 1):
        gate = [
            rad_ref[pl.ds(pair * BLOCK * 8 + level, BLOCK, stride=8), :]
            * env_ref[pair * BLOCK : (pair + 1) * BLOCK, :]
            for pair in range(PAIRS)
        ]
        for dest in range(2):
            for src in range(2):
                block = sum(
                    jnp.where(pair_ref[0, pair] * 2 + pair_ref[1, pair] == dest * 2 + src, 1.0, 0.0) * gate[pair]
                    for pair in range(PAIRS)
                )
                rows, cols = slice(dest * BLOCK, (dest + 1) * BLOCK), slice(src * BLOCK, (src + 1) * BLOCK)
                g_ref[level, rows, cols] = block.astype(BF)
                gt_ref[level, cols, rows] = block.T.astype(BF)


def layer_kernel(
    pair_ref, order_ref, dist_ref, mask_ref, radial_ref, feat_hbm, cot_hbm, w_hbm, v_hbm, u_hbm, o_ref,
    x_ref, cot_ref, h_ref, p_ref, w_ref, v_ref, g_ref, gt_ref, k_ref, turn_ref, rad_ref, env_ref,
    mix_acc, out_acc, grads, ra, sb, rb, sc, own, rc, fin,
    f_s, h_s, h_r, i_s, cot_s, w_s, u_s, a_s, a_r, b_s, b_r, c_s, c_r, d_s, d_r, e_s, e_r,
):
    z, xl, core = lax.axis_index("z"), lax.axis_index("xl"), lax.axis_index("core")
    y, xh = lax.axis_index("y"), lax.axis_index("xh")
    x = xh * 2 + xl
    levels = range(LMAX, -1, -1)

    def copy_a(level):
        return remote(
            grads.at[1 - core, pl.ds(level * C, C)], ra.at[level], a_s.at[level], a_r.at[level], {"core": 1 - core}
        )

    def copy_b(level, j):
        to = lax.rem(y + j, 4)
        return remote(
            sb.at[level, pl.ds(pl.multiple_of(to * 128, 128), 128)],
            rb.at[level, j - 1],
            b_s.at[level, j - 1],
            b_r.at[level, j - 1],
            {"y": to},
        )

    def copy_c(level, k):
        to_z, to_x = lax.rem(z + k // 4, 4), lax.rem(x + k % 4, 4)
        return remote(
            sc.at[level, pl.ds(pl.multiple_of(to_z * 32, 32), 32), pl.ds(pl.multiple_of(to_x * 128, 128), 128)],
            rc.at[level, k - 1],
            c_s.at[level, k - 1],
            c_r.at[level, k - 1],
            {"z": to_z, "xl": lax.rem(to_x, 2), "xh": to_x // 2},
        )

    me = (z * 2 + xl) * 2 + core

    def part(level):
        return pl.ds(level * level * C, (2 * level + 1) * C)

    def copy_h(level, k):
        to = lax.rem(me + k, 16)
        return remote(
            h_ref.at[pl.ds(pl.multiple_of(to * 16, 16), 16), part(level)],
            x_ref.at[pl.ds(pl.multiple_of(me * 16, 16), 16), part(level)],
            h_s.at[level, k - 1],
            h_r.at[level, k - 1],
            {"z": to // 4, "xl": lax.rem(to // 2, 2), "core": lax.rem(to, 2)},
        )

    def stay_h(level):
        rows = pl.ds(pl.multiple_of(me * 16, 16), 16)
        return pltpu.make_async_copy(h_ref.at[rows, part(level)], x_ref.at[rows, part(level)], i_s.at[level])

    cot_in = pltpu.make_async_copy(cot_hbm, cot_ref, cot_s)
    w_in = pltpu.make_async_copy(w_hbm, w_ref, w_s.at[0])
    v_in = pltpu.make_async_copy(v_hbm, v_ref, w_s.at[1])

    def copy_u(level):
        return pltpu.make_async_copy(x_ref.at[:, part(level)], u_hbm.at[:, part(level)], u_s.at[level])

    def copy_f(level):
        return pltpu.make_async_copy(feat_hbm.at[:, part(level)], cot_ref.at[:, part(level)], f_s.at[level])

    def comp_columns(comp):
        return pl.ds(pl.multiple_of(comp * C, C), C)

    for level in levels:
        copy_f(level).start()
    v_in.start()
    w_in.start()
    barrier = pltpu.get_barrier_semaphore()
    friends = [{"y": lax.rem(y + k, 4)} for k in range(1, 4)]
    for k in range(1, 16):
        to = lax.rem(me + k, 16)
        friends.append({"z": to // 4, "xl": lax.rem(to // 2, 2), "core": lax.rem(to, 2)})
    for k in range(8):
        friends.append({"z": lax.rem(z + k // 2, 4), "xl": k % 2, "xh": 1 - xh})
    for where in friends:
        pl.semaphore_signal(barrier, inc=1, device_id=where, device_id_type=MESH)
    row = lax.broadcasted_iota(jnp.int32, (ROWS, ROWS), 0)
    p_ref[...] = jnp.where(row == order_ref[...], 1.0, 0.0).astype(F32).T.astype(BF)

    def ordered(comp, carry):
        cols = comp_columns(comp)
        h_ref[:, cols] = mm(p_ref[...], cot_ref[:, cols]).astype(BF)
        return carry

    for level in levels:
        copy_f(level).wait()
        lax.fori_loop(level * level, (level + 1) * (level + 1), ordered, 0)
        if level == LMAX:
            pl.semaphore_wait(barrier, len(friends))
        for k in range(1, 16):
            copy_h(level, k).start()
        stay_h(level).start()
    cot_in.start()

    gate_sums(dist_ref, radial_ref, turn_ref, k_ref, rad_ref)
    gate_blocks(pair_ref, dist_ref, mask_ref, env_ref, rad_ref, g_ref, gt_ref)
    cot_in.wait()
    v_in.wait()
    w_in.wait()

    def finish_a(level):
        copy_a(level).wait()
        sb[level] = (grads[core, pl.ds(level * C, C)].astype(F32) + ra[level].astype(F32)).astype(BF)
        for j in (2, 1, 3):
            copy_b(level, j).start()

    def finish_b(level):
        for j in (1, 3, 2):
            copy_b(level, j).wait()
        rows = pl.multiple_of(y * 128, 128)
        total = grads[core, pl.ds(level * C + rows, 128)].astype(F32) + ra[level, pl.ds(rows, 128)].astype(F32)
        for j in range(3):
            total = total + rb[level, j].astype(F32)
        own[level] = total
        sc[level] = total.astype(BF)
        for k in range(1, 16):
            copy_c(level, k).start()

    def piece(level, act):
        group = level * 16 + y * 4 + z
        blk = group // 10
        to_y, to_xh = blk // 2, lax.rem(blk, 2)
        rows = pl.multiple_of(lax.rem(group, 10) * 32, 32)
        dst = o_ref.at[core, pl.ds(rows, 32), pl.ds(pl.multiple_of(x * 128, 128), 128)]
        here = jnp.logical_and(to_y == y, to_xh == xh)
        for k in range(8):
            where = {"z": lax.rem(z + k // 2, 4), "xl": lax.rem(xl + k % 2, 2), "y": to_y, "xh": to_xh}
            copy = remote(fin.at[level], dst, d_s.at[level, k], d_r, where)
            if k:
                act(copy)
            else:
                pl.when(jnp.logical_not(here))(lambda: act(copy))
        return here, dst

    def finish_c(level):
        total = own[level, pl.ds(pl.multiple_of(z * 32, 32), 32), pl.ds(pl.multiple_of(x * 128, 128), 128)]
        for k in range(1, 16):
            copy_c(level, k).wait()
            total = total + rc[level, k - 1].astype(F32)
        fin[level] = total
        here, dst = piece(level, lambda copy: copy.start())
        pl.when(here)(lambda: pltpu.make_async_copy(fin.at[level], dst, d_r).start())

    for level in levels:
        stay_h(level).wait()
        for k in range(1, 16):
            copy_h(level, k).wait_recv()
        mix_acc[...] = jnp.zeros_like(mix_acc)
        out_acc[...] = jnp.zeros_like(out_acc)

        def forward(comp, carry):
            cols = comp_columns(comp)
            hidden = x_ref[:, cols]
            source = mm(hidden, w_ref[pl.ds(level * C, C), :]).astype(BF)
            message = mm(g_ref[level], source).astype(BF)
            mixed = mm(message, v_ref[pl.ds(level * C, C), :])
            cot = cot_ref[:, cols]
            out_acc[...] += mm_at(message, cot)
            dmessage = mm_bt(cot, v_ref[pl.ds(level * C, C), :]).astype(BF)
            mix_acc[...] += mm_at(hidden, mm(gt_ref[level], dmessage).astype(BF))
            x_ref[:, cols] = (hidden.astype(F32) + mixed).astype(BF)
            return carry

        lax.fori_loop(level * level, (level + 1) * (level + 1), forward, 0)
        copy_u(level).start()
        grads[0, pl.ds(level * C, C)] = mix_acc[...].astype(BF)
        grads[1, pl.ds(level * C, C)] = out_acc[...].astype(BF)
        copy_a(level).start()
        if level < LMAX:
            finish_a(level + 1)
        if level < LMAX - 1:
            finish_b(level + 2)
        if level < LMAX - 2:
            finish_c(level + 3)
    finish_a(0)
    finish_b(1)
    finish_c(2)
    finish_b(0)
    finish_c(1)
    finish_c(0)
    pltpu.make_async_copy(o_ref.at[core], o_ref.at[core], d_r).wait()
    last = remote(o_ref.at[core], o_ref.at[core], e_s, e_r, {"core": 1 - core})
    last.start()
    for level in levels:
        piece(level, lambda copy: copy.wait_send())
    last.wait()
    for level in levels:
        copy_u(level).wait()
        for k in range(1, 16):
            copy_h(level, k).wait_send()


def run_layer(pair_index, order, dist, mask, radial, features, cotangent, mix_weight, out_weight):
    dma = pltpu.SemaphoreType.DMA
    n = LMAX + 1
    vmem, hbm = pl.BlockSpec(memory_space=pltpu.VMEM), pl.BlockSpec(memory_space=pl.ANY)
    updated, full = pl.pallas_call(
        layer_kernel,
        name="layer",
        out_shape=(
            jax.ShapeDtypeStruct((ROWS, LDEG * C), BF),
            jax.ShapeDtypeStruct((2, 320, C), F32),
        ),
        in_specs=[pl.BlockSpec(memory_space=pltpu.SMEM), vmem, vmem, vmem, vmem, hbm, hbm, hbm, hbm],
        out_specs=(hbm, vmem),
        scratch_shapes=[
            pltpu.VMEM((ROWS, LDEG * C), BF),
            pltpu.VMEM((ROWS, LDEG * C), BF),
            pltpu.VMEM((ROWS, LDEG * C), BF),
            pltpu.VMEM((ROWS, ROWS), BF),
            pltpu.VMEM((WROWS, C), BF),
            pltpu.VMEM((WROWS, C), BF),
            pltpu.VMEM((n, ROWS, ROWS), BF),
            pltpu.VMEM((n, ROWS, ROWS), BF),
            pltpu.VMEM((NRBF, BLOCK), F32),
            pltpu.VMEM((8, NRBF), F32),
            pltpu.VMEM((EDGE_ROWS * 8, BLOCK), F32),
            pltpu.VMEM((EDGE_ROWS, BLOCK), F32),
            pltpu.VMEM((C, C), F32),
            pltpu.VMEM((C, C), F32),
            pltpu.VMEM((2, WROWS, C), BF),
            pltpu.VMEM((n, C, C), BF),
            pltpu.VMEM((n, C, C), BF),
            pltpu.VMEM((n, 3, 128, C), BF),
            pltpu.VMEM((n, 128, C), BF),
            pltpu.VMEM((n, 128, C), F32),
            pltpu.VMEM((n, 15, 32, 128), BF),
            pltpu.VMEM((n, 32, 128), F32),
            dma((n,)),
            dma((n, 15)),
            dma((n, 15)),
            dma((n,)),
            dma,
            dma((2,)),
            dma((n,)),
            dma((n,)),
            dma((n,)),
            dma((n, 3)),
            dma((n, 3)),
            dma((n, 15)),
            dma((n, 15)),
            dma((n, 8)),
            dma,
            dma,
            dma,
        ],
        compiler_params=pltpu.CompilerParams(collective_id=0, has_side_effects=True, vmem_limit_bytes=VM),
    )(pair_index, order, dist, mask, radial, features, cotangent, mix_weight, out_weight)
    return updated, full[0], full[1]


def body(
    features,
    cotangent,
    send_order,
    pair_index,
    edge_mask,
    distance,
    radial_weight,
    mix_weight,
    out_weight,
):
    dist = distance.reshape(EDGE_ROWS, BLOCK)
    mask = edge_mask.reshape(EDGE_ROWS, BLOCK)
    return run_layer(
        pair_index.T, send_order, dist, mask, radial_weight.T, features, cotangent, mix_weight, out_weight
    )


def solution(mesh):
    split = Mesh(mesh.devices.reshape(4, 2, 2, 4, 2), DP + BLK)
    rows = P(DP + BLK, None)
    cubes = P(DP + BLK, None, None)
    return jax.shard_map(
        body,
        mesh=split,
        in_specs=(rows, rows, rows, rows, cubes, cubes, P(), P(), P()),
        out_specs=(rows, P(BLK, None), P(BLK, None)),
        check_vma=False,
    )
```

```python
import math

import jax
import jax.numpy as jnp
from jax import lax
from jax.experimental import pallas as pl
from jax.experimental.pallas import tpu as pltpu
from jax.sharding import Mesh
from jax.sharding import PartitionSpec as P

LMAX = 4
LDEG = 25
BLOCK = 128
PAIRS = 3
NRBF = 512
C = 512
ROWS = 256
EDGE_ROWS = PAIRS * BLOCK
CHUNKS = ((0, 1), (1, 4), (4, 9), (9, 16), (16, 19), (19, 22), (22, 25))
WROWS = 2560
DP = ("z", "xl", "core")
BLK = ("y", "xh")
MESH = pl.DeviceIdType.MESH

edge_scale = 0.25
cut_radius = 5.0

BF = jnp.bfloat16
F32 = jnp.float32
VM = 62 << 20


def mm(a, b):
    return jnp.dot(a, b, preferred_element_type=F32)


def mm_bt(a, b):
    return lax.dot_general(a, b, (((1,), (1,)), ((), ())), preferred_element_type=F32)


def mm_at(a, b):
    return lax.dot_general(a, b, (((0,), (0,)), ((), ())), preferred_element_type=F32)


def remote(src, dst, send, recv, where):
    return pltpu.make_async_remote_copy(
        src_ref=src, dst_ref=dst, send_sem=send, recv_sem=recv, device_id=where, device_id_type=MESH
    )


def gate_sums(dist_ref, radial_ref, turn_ref, k_ref, rad_ref):
    scale = math.sqrt(0.5 * math.log2(math.e))
    k_ref[...] = lax.broadcasted_iota(jnp.int32, (NRBF, BLOCK), 0).astype(F32) * scale
    turn_ref[...] = jnp.zeros_like(turn_ref)
    turn_ref[: LMAX + 1, :] = radial_ref[...]
    radial = turn_ref[...]
    high_w = radial.astype(BF)
    low_w = (radial - high_w.astype(F32)).astype(BF)
    weight = jnp.concatenate(
        [
            jnp.concatenate([high_w, high_w], axis=1).astype(F32),
            jnp.concatenate([low_w, jnp.zeros_like(low_w)], axis=1).astype(F32),
        ],
        axis=0,
    ).astype(BF)

    def step(at, carry):
        base = at * 8
        rows = dist_ref[pl.ds(pl.multiple_of(base, 8), 8), :] * ((NRBF - 1) / cut_radius * scale)
        for two in range(4):
            high, low = [], []
            for one in range(2):
                spot = two * 2 + one
                off = rows[spot : spot + 1, :] - k_ref[...]
                basis = jnp.exp2(-(off * off))
                top = basis.astype(BF)
                high.append(top)
                low.append((basis - top.astype(F32)).astype(BF))
            both = mm(weight, jnp.concatenate([jnp.concatenate(high, axis=1), jnp.concatenate(low, axis=1)], axis=0))
            total = both[:8] + both[8:]
            for one in range(2):
                spot = two * 2 + one
                rad_ref[pl.ds(pl.multiple_of((base + spot) * 8, 8), 8), :] = total[
                    :, one * BLOCK : (one + 1) * BLOCK
                ]
        return carry

    lax.fori_loop(0, EDGE_ROWS // 8, step, 0)


def gate_blocks(pair_ref, dist_ref, mask_ref, env_ref, rad_ref, g_ref, gt_ref):
    env_ref[...] = (
        0.5 * (jnp.cos(math.pi * dist_ref[...] / cut_radius) + 1.0) * mask_ref[...].astype(F32) * edge_scale
    )
    for level in range(LMAX + 1):
        gate = [
            rad_ref[pl.ds(pair * BLOCK * 8 + level, BLOCK, stride=8), :]
            * env_ref[pair * BLOCK : (pair + 1) * BLOCK, :]
            for pair in range(PAIRS)
        ]
        for dest in range(2):
            for src in range(2):
                block = sum(
                    jnp.where(pair_ref[0, pair] * 2 + pair_ref[1, pair] == dest * 2 + src, 1.0, 0.0) * gate[pair]
                    for pair in range(PAIRS)
                )
                rows, cols = slice(dest * BLOCK, (dest + 1) * BLOCK), slice(src * BLOCK, (src + 1) * BLOCK)
                g_ref[level, rows, cols] = block.astype(BF)
                gt_ref[level, cols, rows] = block.T.astype(BF)


def layer_kernel(
    pair_ref, order_ref, dist_ref, mask_ref, radial_ref, feat_hbm, cot_hbm, w_hbm, v_hbm, u_hbm, mix_ref, out_ref,
    x_ref, cot_ref, h_ref, p_ref, w_ref, v_ref, g_ref, gt_ref, k_ref, turn_ref, rad_ref, env_ref,
    mix_acc, out_acc, grads, ra, sb, rb, sc, own, rc, fin, o_ref,
    f_s, h_s, h_r, i_s, cot_s, w_s, u_s, a_s, a_r, b_s, b_r, c_s, c_r, d_s, d_r, e_s, e_r,
):
    z, xl, core = lax.axis_index("z"), lax.axis_index("xl"), lax.axis_index("core")
    y, xh = lax.axis_index("y"), lax.axis_index("xh")
    x = xh * 2 + xl
    levels = range(LMAX + 1)
    chunks = range(len(CHUNKS))

    def copy_a(level):
        return remote(
            grads.at[1 - core, pl.ds(level * C, C)], ra.at[level], a_s.at[level], a_r.at[level], {"core": 1 - core}
        )

    def copy_b(level, j):
        to = lax.rem(y + j, 4)
        return remote(
            sb.at[level, pl.ds(pl.multiple_of(to * 128, 128), 128)],
            rb.at[level, j - 1],
            b_s.at[level, j - 1],
            b_r.at[level, j - 1],
            {"y": to},
        )

    def copy_c(level, k):
        to_z, to_x = lax.rem(z + k // 4, 4), lax.rem(x + k % 4, 4)
        return remote(
            sc.at[level, pl.ds(pl.multiple_of(to_z * 32, 32), 32), pl.ds(pl.multiple_of(to_x * 128, 128), 128)],
            rc.at[level, k - 1],
            c_s.at[level, k - 1],
            c_r.at[level, k - 1],
            {"z": to_z, "xl": lax.rem(to_x, 2), "xh": to_x // 2},
        )

    me = (z * 2 + xl) * 2 + core

    def part(chunk):
        first, last = CHUNKS[chunk]
        return pl.ds(first * C, (last - first) * C)

    def copy_h(chunk, k):
        to = lax.rem(me + k, 16)
        return remote(
            h_ref.at[pl.ds(pl.multiple_of(to * 16, 16), 16), part(chunk)],
            x_ref.at[pl.ds(pl.multiple_of(me * 16, 16), 16), part(chunk)],
            h_s.at[chunk, k - 1],
            h_r.at[chunk, k - 1],
            {"z": to // 4, "xl": lax.rem(to // 2, 2), "core": lax.rem(to, 2)},
        )

    def stay_h(chunk):
        rows = pl.ds(pl.multiple_of(me * 16, 16), 16)
        return pltpu.make_async_copy(h_ref.at[rows, part(chunk)], x_ref.at[rows, part(chunk)], i_s.at[chunk])

    cot_in = pltpu.make_async_copy(cot_hbm, cot_ref, cot_s)
    w_in = pltpu.make_async_copy(w_hbm, w_ref, w_s.at[0])
    v_in = pltpu.make_async_copy(v_hbm, v_ref, w_s.at[1])

    def copy_u(chunk):
        return pltpu.make_async_copy(x_ref.at[:, part(chunk)], u_hbm.at[:, part(chunk)], u_s.at[chunk])

    def copy_f(chunk):
        return pltpu.make_async_copy(feat_hbm.at[:, part(chunk)], cot_ref.at[:, part(chunk)], f_s.at[chunk])

    def comp_columns(comp):
        return pl.ds(pl.multiple_of(comp * C, C), C)

    for chunk in chunks:
        copy_f(chunk).start()
    v_in.start()
    w_in.start()
    barrier = pltpu.get_barrier_semaphore()
    friends = [{"y": lax.rem(y + k, 4)} for k in range(1, 4)]
    for k in range(1, 16):
        to = lax.rem(me + k, 16)
        friends.append({"z": to // 4, "xl": lax.rem(to // 2, 2), "core": lax.rem(to, 2)})
    for k in range(8):
        friends.append({"z": lax.rem(z + k // 2, 4), "xl": k % 2, "xh": 1 - xh})
    for where in friends:
        pl.semaphore_signal(barrier, inc=1, device_id=where, device_id_type=MESH)
    row = lax.broadcasted_iota(jnp.int32, (ROWS, ROWS), 0)
    p_ref[...] = jnp.where(row == order_ref[...], 1.0, 0.0).astype(F32).T.astype(BF)

    def ordered(comp, carry):
        cols = comp_columns(comp)
        h_ref[:, cols] = mm(p_ref[...], cot_ref[:, cols]).astype(BF)
        return carry

    for chunk in chunks:
        copy_f(chunk).wait()
        lax.fori_loop(*CHUNKS[chunk], ordered, 0)
        if chunk == 0:
            pl.semaphore_wait(barrier, len(friends))
        for k in range(1, 16):
            copy_h(chunk, k).start()
        stay_h(chunk).start()
    cot_in.start()

    gate_sums(dist_ref, radial_ref, turn_ref, k_ref, rad_ref)
    gate_blocks(pair_ref, dist_ref, mask_ref, env_ref, rad_ref, g_ref, gt_ref)
    cot_in.wait()
    v_in.wait()
    w_in.wait()

    def finish_a(level):
        copy_a(level).wait()
        sb[level] = (grads[core, pl.ds(level * C, C)].astype(F32) + ra[level].astype(F32)).astype(BF)
        for j in (2, 1, 3):
            copy_b(level, j).start()

    def finish_b(level):
        for j in (1, 3, 2):
            copy_b(level, j).wait()
        rows = pl.multiple_of(y * 128, 128)
        total = grads[core, pl.ds(level * C + rows, 128)].astype(F32) + ra[level, pl.ds(rows, 128)].astype(F32)
        for j in range(3):
            total = total + rb[level, j].astype(F32)
        own[level] = total
        sc[level] = total.astype(BF)
        for k in range(1, 16):
            copy_c(level, k).start()

    def piece(level, act):
        group = level * 16 + y * 4 + z
        blk = group // 10
        to_y, to_xh = blk // 2, lax.rem(blk, 2)
        rows = pl.multiple_of(lax.rem(group, 10) * 32, 32)
        dst = o_ref.at[core, pl.ds(rows, 32), pl.ds(pl.multiple_of(x * 128, 128), 128)]
        here = jnp.logical_and(to_y == y, to_xh == xh)
        for k in range(8):
            where = {"z": lax.rem(z + k // 2, 4), "xl": lax.rem(xl + k % 2, 2), "y": to_y, "xh": to_xh}
            copy = remote(fin.at[level], dst, d_s.at[level, k], d_r, where)
            if k:
                act(copy)
            else:
                pl.when(jnp.logical_not(here))(lambda: act(copy))
        return here, dst

    def finish_c(level):
        total = own[level, pl.ds(pl.multiple_of(z * 32, 32), 32), pl.ds(pl.multiple_of(x * 128, 128), 128)]
        for k in range(1, 16):
            copy_c(level, k).wait()
            total = total + rc[level, k - 1].astype(F32)
        fin[level] = total.astype(BF)
        here, dst = piece(level, lambda copy: copy.start())
        pl.when(here)(lambda: pltpu.make_async_copy(fin.at[level], dst, d_r).start())

    def arrive(chunk):
        stay_h(chunk).wait()
        for k in range(1, 16):
            copy_h(chunk, k).wait_recv()

    def forward(level, first, count, fresh):
        weights = pl.ds(level * C, C)

        def columns(spot):
            return pl.ds(pl.multiple_of((first + spot) * C, C), C)

        def stacked(ref):
            return jnp.concatenate([ref[:, columns(spot)] for spot in range(count)], axis=0)

        def spread(gate, value):
            mixed = [mm(gate, value[spot * ROWS : (spot + 1) * ROWS]).astype(BF) for spot in range(count)]
            return jnp.concatenate(mixed, axis=0)

        hidden, cot = stacked(x_ref), stacked(cot_ref)
        message = spread(g_ref[level], mm(hidden, w_ref[weights, :]).astype(BF))
        out_sum = mm_at(message, cot)
        mixed = mm(message, v_ref[weights, :])
        dmessage = mm_bt(cot, v_ref[weights, :]).astype(BF)
        mix_sum = mm_at(hidden, spread(gt_ref[level], dmessage))
        updated = (hidden.astype(F32) + mixed).astype(BF)
        for spot in range(count):
            x_ref[:, columns(spot)] = updated[spot * ROWS : (spot + 1) * ROWS]
        if fresh:
            out_acc[...] = out_sum
            mix_acc[...] = mix_sum
        else:
            out_acc[...] += out_sum
            mix_acc[...] += mix_sum

    def start_a(level):
        grads[0, pl.ds(level * C, C)] = mix_acc[...].astype(BF)
        grads[1, pl.ds(level * C, C)] = out_acc[...].astype(BF)
        copy_a(level).start()

    def forward_three(level, first, count):
        def step(at, carry):
            forward(level, first + 3 * at, 3, False)
            return carry

        lax.fori_loop(0, count, step, 0)

    arrive(0)
    forward(0, 0, 1, True)
    copy_u(0).start()
    start_a(0)
    arrive(1)
    forward(1, 1, 3, True)
    copy_u(1).start()
    start_a(1)
    finish_a(0)
    arrive(2)
    forward(2, 4, 2, True)
    forward_three(2, 6, 1)
    copy_u(2).start()
    start_a(2)
    finish_a(1)
    finish_b(0)
    arrive(3)
    forward(3, 9, 1, True)
    forward_three(3, 10, 2)
    copy_u(3).start()
    start_a(3)
    finish_a(2)
    finish_b(1)
    mix_acc[...] = jnp.zeros_like(mix_acc)
    out_acc[...] = jnp.zeros_like(out_acc)
    for chunk in (4, 5, 6):
        arrive(chunk)
        forward_three(4, CHUNKS[chunk][0], 1)
        copy_u(chunk).start()
        if chunk == 4:
            finish_a(3)
            finish_b(2)
        if chunk == 5:
            finish_b(3)
    start_a(4)
    finish_a(4)
    for level in range(LMAX):
        finish_c(level)
    finish_b(4)
    finish_c(4)
    pltpu.make_async_copy(o_ref.at[core], o_ref.at[core], d_r).wait()
    last = remote(o_ref.at[core], o_ref.at[core], e_s, e_r, {"core": 1 - core})
    last.start()
    for level in levels:
        piece(level, lambda copy: copy.wait_send())
    last.wait()
    mix_ref[...] = o_ref[0].astype(F32)
    out_ref[...] = o_ref[1].astype(F32)
    for chunk in chunks:
        copy_u(chunk).wait()
        for k in range(1, 16):
            copy_h(chunk, k).wait_send()


def run_layer(pair_index, order, dist, mask, radial, features, cotangent, mix_weight, out_weight):
    dma = pltpu.SemaphoreType.DMA
    n = LMAX + 1
    vmem, hbm = pl.BlockSpec(memory_space=pltpu.VMEM), pl.BlockSpec(memory_space=pl.ANY)
    return pl.pallas_call(
        layer_kernel,
        name="layer",
        out_shape=(
            jax.ShapeDtypeStruct((ROWS, LDEG * C), BF),
            jax.ShapeDtypeStruct((320, C), F32),
            jax.ShapeDtypeStruct((320, C), F32),
        ),
        in_specs=[pl.BlockSpec(memory_space=pltpu.SMEM), vmem, vmem, vmem, vmem, hbm, hbm, hbm, hbm],
        out_specs=(hbm, vmem, vmem),
        scratch_shapes=[
            pltpu.VMEM((ROWS, LDEG * C), BF),
            pltpu.VMEM((ROWS, LDEG * C), BF),
            pltpu.VMEM((ROWS, LDEG * C), BF),
            pltpu.VMEM((ROWS, ROWS), BF),
            pltpu.VMEM((WROWS, C), BF),
            pltpu.VMEM((WROWS, C), BF),
            pltpu.VMEM((n, ROWS, ROWS), BF),
            pltpu.VMEM((n, ROWS, ROWS), BF),
            pltpu.VMEM((NRBF, BLOCK), F32),
            pltpu.VMEM((8, NRBF), F32),
            pltpu.VMEM((EDGE_ROWS * 8, BLOCK), F32),
            pltpu.VMEM((EDGE_ROWS, BLOCK), F32),
            pltpu.VMEM((C, C), F32),
            pltpu.VMEM((C, C), F32),
            pltpu.VMEM((2, WROWS, C), BF),
            pltpu.VMEM((n, C, C), BF),
            pltpu.VMEM((n, C, C), BF),
            pltpu.VMEM((n, 3, 128, C), BF),
            pltpu.VMEM((n, 128, C), BF),
            pltpu.VMEM((n, 128, C), F32),
            pltpu.VMEM((n, 15, 32, 128), BF),
            pltpu.VMEM((n, 32, 128), BF),
            pltpu.VMEM((2, 320, C), BF),
            dma((len(CHUNKS),)),
            dma((len(CHUNKS), 15)),
            dma((len(CHUNKS), 15)),
            dma((len(CHUNKS),)),
            dma,
            dma((2,)),
            dma((len(CHUNKS),)),
            dma((n,)),
            dma((n,)),
            dma((n, 3)),
            dma((n, 3)),
            dma((n, 15)),
            dma((n, 15)),
            dma((n, 8)),
            dma,
            dma,
            dma,
        ],
        compiler_params=pltpu.CompilerParams(collective_id=0, has_side_effects=True, vmem_limit_bytes=VM),
    )(pair_index, order, dist, mask, radial, features, cotangent, mix_weight, out_weight)


def body(
    features,
    cotangent,
    send_order,
    pair_index,
    edge_mask,
    distance,
    radial_weight,
    mix_weight,
    out_weight,
):
    dist = distance.reshape(EDGE_ROWS, BLOCK)
    mask = edge_mask.reshape(EDGE_ROWS, BLOCK)
    return run_layer(
        pair_index.T, send_order, dist, mask, radial_weight.T, features, cotangent, mix_weight, out_weight
    )


def solution(mesh):
    split = Mesh(mesh.devices.reshape(4, 2, 2, 4, 2), DP + BLK)
    rows = P(DP + BLK, None)
    cubes = P(DP + BLK, None, None)
    return jax.shard_map(
        body,
        mesh=split,
        in_specs=(rows, rows, rows, rows, cubes, cubes, P(), P(), P()),
        out_specs=(rows, P(BLK, None), P(BLK, None)),
        check_vma=False,
    )
```
